512 devices in a mesh: row: 16 (over z_lo, y), col: 32 (over z_hi, x, core).
Axes of the slice: x: 4, y: 4, z: 16 (z_hi: 4, z_lo: 4; z = z_hi * 4 + z_lo), core: 2. Of those that a mesh axis runs over, the one named last changes fastest.
Arguments:
- ancestor: float32 [20480, 20480], P('row', 'col'), as said below
- factor_rows: float32 [2, 256, 20480], P(None, 'row', 'col'), may hold values from -6 to 6
- block_lists: int32 [2, 8], replicated, may hold values from 0 to 15, as said below
Outputs:
- inverse_panel: float32 [2, 20480, 256], P(None, ('row', 'col'))
- inverse_rows: float32 [2, 256, 20480], P(None, 'col', 'row')
The draws below stay inside these ranges and needn't reach their ends.
Inputs may be any that keep to these rules, and one draw needn't show every extreme that they name: `block_lists`: each row lists 8 distinct blocks in increasing order; the first block 0 and the last block 15 are in every row. ancestor is symmetric: ancestor[i, j] = ancestor[j, i].
All inputs are finite; a program needn't handle non-finite values.
Results may differ from the reference program's by a relative error of at most 0.000071.
Values sent between devices are 32-bit elements; how exact they have to be, the bound alone decides.
A program may use at most 64 MiB of HBM per device.

```python
import math
import jax
import jax.numpy as jnp
from jax import lax

W = 256
BS = 1280
NB = 16
NLIST = 8
SIB = 2
NA = 20480


def draw_block_lists(key, part):
    chosen = []
    for member in range(SIB):
        shuffled = jax.random.permutation(jax.random.fold_in(key, member + 17), NB - 2)[:NLIST - 2]
        middle = (shuffled.astype(jnp.int32) + 1).astype(jnp.int32)
        picked = jnp.concatenate([jnp.zeros((1,), jnp.int32), middle, jnp.full((1,), NB - 1, jnp.int32)])
        chosen.append(jnp.sort(picked))
    return jnp.stack(chosen).astype(jnp.int32)


def draw_ancestor(key, part):
    base = jax.random.normal(jax.random.fold_in(key, 3), (NA, NA), jnp.float32)
    symmetric = jnp.clip((base + base.T) * math.sqrt(0.5), -6.0, 6.0)
    return symmetric * NA ** (-0.5)


def block_scale(stream_key, shape, pieces, low, top_value):
    factor_of = 1.0
    for axis_at, shards_of in pieces:
        heights = jax.random.uniform(jax.random.fold_in(jax.random.fold_in(stream_key, 6), axis_at), (shards_of,), jnp.float32, low / len(pieces), top_value / len(pieces))
        factor_of = factor_of * jnp.repeat(jnp.exp(heights), shape[axis_at] // shards_of).reshape((-1,) + (1,) * (len(shape) - 1 - axis_at))
    return factor_of


def gaussian(key, extent, width, bound, split=(), kind=jnp.bfloat16):
    result = jax.random.normal(key, extent, jnp.float32) * width
    if len(split) > 0:
        result = block_scale(key, extent, split, -0.22, 0.18) * result
    return jnp.clip(result, min=-bound, max=bound).astype(kind)


def setup_inputs(seed: int = 0) -> dict:
    seeds = jax.random.split(jax.random.key(seed), 4)
    ancestor = draw_ancestor(jax.random.fold_in(seeds[3], 71), 0)
    factor_rows = gaussian(seeds[1], (SIB, W, NA), 1.0, 6.0, ((1, 16), (2, 32)), jnp.float32)
    block_lists = draw_block_lists(jax.random.fold_in(seeds[3], 71), 0)
    return {"ancestor": ancestor, "factor_rows": factor_rows, "block_lists": block_lists}


def listed_mask(block_lists, blocks):
    return jnp.any(block_lists[:, :, None] == blocks[None, None, :], axis=1).astype(jnp.float32)


def reference(ancestor, factor_rows, block_lists):
    blocks = (jnp.arange(NB * BS, dtype=jnp.int32) // BS).astype(jnp.int32)
    listed = listed_mask(block_lists, blocks)
    masked = factor_rows * listed[:, None, :]
    product = jnp.einsum("ij,swj->siw", ancestor, masked, precision=lax.Precision.HIGHEST)
    inverse_panel = -product * listed[:, :, None]
    inverse_rows = jnp.transpose(inverse_panel, (0, 2, 1))
    return inverse_panel, inverse_rows
```

```python
import jax
import jax.numpy as jnp
from jax import lax
from jax.experimental import pallas as pl
from jax.experimental.pallas import tpu as pltpu
from jax.sharding import PartitionSpec as P

MESH = pl.DeviceIdType.MESH
F32 = jnp.float32
BF16 = jnp.bfloat16
NT = (((1,), (1,)), ((), ()))
ORDER = (2, 1, 3, 0)


def kernel(
    lists, a_hbm, f_hbm, panel, rows,
    a_v, ah, al, fbuf, fcat, ybuf, xr, zr, tin, tbuf, rbuf, pbuf,
    a_sem, ap_sem, ap_send, g_recv, g_send, x_recv, x_send, z_recv, z_send,
    t_recv, t_send, p_recv, p_send,
):
    r = lax.axis_index("row")
    c = lax.axis_index("col")
    zl, y = r // 4, r % 4
    zh, x, k = c // 8, (c // 2) % 4, c % 2
    o_k = 1 - k

    def dev(zl_, y_, zh_, x_, k_):
        return (zl_ * 4 + y_, zh_ * 8 + x_ * 2 + k_)

    partner = dev(zl, y, zh, x, o_k)
    yp, ym = (y + 1) % 4, (y + 3) % 4
    xp, xm, xo = (x + 1) % 4, (x + 3) % 4, (x + 2) % 4
    zp, zm = (zh + 1) % 4, (zh + 3) % 4

    barrier = pltpu.get_barrier_semaphore()
    near = [partner]
    for kk in range(2):
        near += [dev(zl, yp, zh, x, kk), dev(zl, ym, zh, x, kk)]
        near += [dev((zl + t) % 4, y, zh, x, kk) for t in (1, 2, 3)]
    near += [dev(zl, y, zh, xp, k), dev(zl, y, zh, xm, k)]
    near += [dev(zl, y, zp, x, k), dev(zl, y, zm, x, k)]
    for d in near:
        pl.semaphore_signal(barrier, inc=1, device_id=d, device_id_type=MESH)
    pl.semaphore_wait(barrier, len(near))

    sends = []

    def rcopy(src, dst, ssem, rsem, to, when=None):
        d = pltpu.make_async_remote_copy(
            src_ref=src, dst_ref=dst, send_sem=ssem, recv_sem=rsem,
            device_id=to, device_id_type=MESH)
        if when is None:
            d.start()
        else:
            pl.when(when)(d.start)
        sends.append((d, when))
        return d

    def got(dst, sem):
        pltpu.make_async_copy(dst, dst, sem).wait()

    kd = zl // 2
    m_src = jnp.where(kd == 0, zl, 3 - zl)
    own = (r - 8 * kd) * 16
    cols_k = pl.ds(pl.multiple_of(k * 640, 128), 640)

    def seg(kk, m):
        return jnp.where(kk == 0, m, 3 - m)

    own_rows = pl.ds(pl.multiple_of(own, 16), 16)
    g_i = [0]

    def gsem():
        g_i[0] += 1
        return g_send.at[g_i[0] - 1]

    local = []
    for s in range(2):
        dst = fbuf.at[s, own_rows, cols_k]
        sem = g_recv.at[s, r - 8 * kd, k]
        for to in (
            dev(seg(kd, 2), y, zh, x, kd),
            dev(seg(kd, 1 - m_src), y, zh, x, kd),
            dev(zl, yp, zh, x, kd),
            dev(zl, ym, zh, x, kd),
        ):
            rcopy(f_hbm.at[s], dst, gsem(), sem, to)
        rcopy(f_hbm.at[s], dst, gsem(), sem, partner, when=k != kd)
        cp = pltpu.make_async_copy(f_hbm.at[s], dst, sem)
        pl.when(k == kd)(cp.start)

    for q in range(4):
        rq = pl.ds(q * 320, 320)
        pltpu.make_async_copy(a_hbm.at[rq, :], a_v.at[rq, cols_k], a_sem.at[q]).start()
        rcopy(a_hbm.at[rq, :], a_v.at[rq, cols_k], ap_send.at[q], ap_sem.at[q], partner)

    m = seg(k, zl)
    end = dev(seg(k, 3), y, zh, x, k)

    def slot(mp, yy):
        return seg(k, mp) * 4 + yy - 8 * k

    def half(s, sl, h):
        return fbuf.at[s, pl.ds(pl.multiple_of(sl * 16, 16), 16), pl.ds(h * 640, 640)]

    def part(s, sl, h):
        return fbuf.at[s, pl.ds(pl.multiple_of(sl * 16 + h * 8, 8), 8), :]

    def gather_z(s):
        for mp in (1, 0):
            sl = slot(mp, y)
            for h in range(2):
                piece = half(s, sl, h)
                got(piece, g_recv.at[s, sl, h])
                rcopy(piece, piece, gsem(), g_recv.at[s, sl, h], end, when=m == 2)
                for yy in (yp, ym):
                    rcopy(piece, piece, gsem(), g_recv.at[s, sl, h],
                          dev(zl, yy, zh, x, k), when=m != mp)

    def gather_y(s):
        for mp in (1, 0):
            for side, (yy, to) in enumerate(((ym, yp), (yp, ym))):
                sl = slot(mp, yy)
                for h in range(2):
                    got(half(s, sl, h), g_recv.at[s, sl, h])
                piece = part(s, sl, side)
                rcopy(piece, piece, gsem(), g_recv.at[s, sl, side], dev(zl, to, zh, x, k))

    def gather_end(s):
        for mp in (1, 0):
            sl = slot(mp, (y + 2) % 4)
            for h in range(2):
                got(part(s, sl, h), g_recv.at[s, sl, h])

    cb = zh * 4 + x

    def listed(s, b):
        hit = lists[s, 0] == b
        for t in range(1, 8):
            hit = jnp.logical_or(hit, lists[s, t] == b)
        return jnp.where(hit, 1.0, 0.0).astype(F32)

    def split_a():
        for q in range(4):
            rq = pl.ds(q * 320, 320)
            got(a_v.at[rq, cols_k], a_sem.at[q])
            got(a_v.at[rq, pl.ds(pl.multiple_of(o_k * 640, 128), 640)], ap_sem.at[q])

            def step(t, _):
                at = pl.ds(pl.multiple_of(q * 320 + t * 32, 32), 32)
                v = a_v[at, :]
                hi = v.astype(BF16)
                ah[at, :] = hi
                al[at, :] = (v - hi.astype(F32)).astype(BF16)
                return 0

            lax.fori_loop(0, 10, step, 0)

    def split_f(s):
        mask = listed(s, cb)
        v = fbuf[s] * mask
        hi = v.astype(BF16)
        fcat[s, 0:128, :] = hi
        fcat[s, 128:256, :] = (v - hi.astype(F32)).astype(BF16)

    def compute(s, o):
        zc = (zh + ORDER[o]) % 4
        at = pl.ds(pl.multiple_of(zc * 320, 320), 320)
        sign = -listed(s, r)
        p1 = lax.dot_general(ah[at, :], fcat[s], NT, preferred_element_type=F32)
        p2 = lax.dot_general(al[at, :], fcat[s, 0:128, :], NT, preferred_element_type=F32)
        ybuf[s, o] = (p1[:, 0:128] + (p1[:, 128:256] + p2)) * sign

    def yp_rows(s, o, xx, h):
        return s, o, pl.ds(pl.multiple_of(xx * 80 + h * 40, 8), 40), slice(None)

    to_xp, to_xm = dev(zl, y, zh, xp, k), dev(zl, y, zh, xm, k)
    to_zp, to_zm = dev(zl, y, zp, x, k), dev(zl, y, zm, x, k)

    def xsend(s, o, kind, xx, h, to):
        rcopy(ybuf.at[yp_rows(s, o, xx, h)], xr.at[s, o, kind],
              x_send.at[s, o, kind], x_recv.at[s, o, kind], to)

    def xgot(s, o, kind):
        got(xr.at[s, o, kind], x_recv.at[s, o, kind])

    def x1(s, o):
        xsend(s, o, 0, xo, 0, to_xp)
        xsend(s, o, 1, xo, 1, to_xm)
        xsend(s, o, 4, xp, 1, to_xp)
        xsend(s, o, 5, xm, 0, to_xm)

    def x2(s, o):
        xgot(s, o, 0)
        i = yp_rows(s, o, xp, 0)
        ybuf[i] = ybuf[i] + xr[s, o, 0]
        xsend(s, o, 2, xp, 0, to_xp)
        xgot(s, o, 1)
        i = yp_rows(s, o, xm, 1)
        ybuf[i] = ybuf[i] + xr[s, o, 1]
        xsend(s, o, 3, xm, 1, to_xm)

    def x3(s, o):
        for kinds, h in (((5, 2), 0), ((4, 3), 1)):
            for kind in kinds:
                xgot(s, o, kind)
            i = yp_rows(s, o, x, h)
            ybuf[i] = ybuf[i] + xr[s, o, kinds[0]] + xr[s, o, kinds[1]]

    def zsend(s, o, kind, h, to):
        rcopy(ybuf.at[yp_rows(s, o, x, h)], zr.at[s, kind],
              z_send.at[s, kind], z_recv.at[s, kind], to)

    def zgot(s, kind):
        got(zr.at[s, kind], z_recv.at[s, kind])

    def zadd(s, o, kind, h):
        zgot(s, kind)
        i = yp_rows(s, o, x, h)
        ybuf[i] = ybuf[i] + zr[s, kind]

    def z_far(s):
        zsend(s, 0, 0, 0, to_zp)
        zsend(s, 0, 1, 1, to_zm)

    def z_direct(s, o):
        if o == 1:
            zsend(s, 1, 4, 1, to_zp)
        else:
            zsend(s, 2, 5, 0, to_zm)

    def z_sum(s, o):
        if o == 1:
            zadd(s, 1, 0, 0)
            zsend(s, 1, 2, 0, to_zp)
        else:
            zadd(s, 2, 1, 1)
            zsend(s, 2, 3, 1, to_zm)

    def finish(s):
        for kinds, h in (((5, 2), 0), ((4, 3), 1)):
            for kind in kinds:
                zgot(s, kind)
            v = ybuf[yp_rows(s, 3, x, h)] + zr[s, kinds[0]] + zr[s, kinds[1]]
            tin[s, pl.ds(h * 40, 40), :] = v
        rcopy(tin.at[s, pl.ds(pl.multiple_of(o_k * 40, 8), 40), :], pbuf.at[s],
              p_send.at[s], p_recv.at[s], partner)
        tin[s, 80:128, :] = jnp.zeros((48, 128), F32)
        tbuf[s] = tin[s].T
        for n in range(16):
            nn = (n + c) % 16
            src = tbuf.at[s, pl.ds(pl.multiple_of(nn * 8, 8), 8), :]
            dst = rbuf.at[s, cb]
            to_c = 16 * k + nn
            rcopy(src, dst, t_send.at[s, n], t_recv.at[s], (r, to_c), when=to_c != c)
            cp = pltpu.make_async_copy(src, dst, t_recv.at[s])
            pl.when(to_c == c)(cp.start)

    def outputs(s):
        panel[s, :, pl.ds(pl.multiple_of(k * 128, 128), 128)] = tin[
            s, pl.ds(pl.multiple_of(k * 40, 8), 40), :]
        got(pbuf.at[s], p_recv.at[s])
        panel[s, :, pl.ds(pl.multiple_of(o_k * 128, 128), 128)] = pbuf[s]
        got(rbuf.at[s], t_recv.at[s])
        lane = lax.broadcasted_iota(jnp.int32, (8, 128), 1)
        tiles = [jnp.zeros((8, 128), F32) for _ in range(10)]
        for n in range(16):
            t, off = (80 * n) // 128, (80 * n) % 128
            v = rbuf[s, n]
            if off:
                v = pltpu.roll(v, off, 1)
            tiles[t] = jnp.where((lane >= off) & (lane < off + 80), v, tiles[t])
            if off + 80 > 128:
                tiles[t + 1] = jnp.where(lane < off + 80 - 128, v, tiles[t + 1])
        for t in range(10):
            rows[s, :, t * 128:(t + 1) * 128] = tiles[t]

    gather_z(0)
    gather_z(1)
    split_a()
    gather_y(0)
    gather_end(0)
    split_f(0)
    compute(0, 0)
    x1(0, 0)
    compute(0, 1)
    x1(0, 1)
    gather_y(1)
    x2(0, 0)
    compute(0, 2)
    x1(0, 2)
    x2(0, 1)
    x3(0, 0)
    z_far(0)
    compute(0, 3)
    x1(0, 3)
    gather_end(1)
    split_f(1)
    compute(1, 0)
    x1(1, 0)
    x2(0, 2)
    x3(0, 1)
    z_direct(0, 1)
    x2(0, 3)
    x3(0, 2)
    z_direct(0, 2)
    compute(1, 1)
    x1(1, 1)
    z_sum(0, 1)
    z_sum(0, 2)
    x3(0, 3)
    x2(1, 0)
    compute(1, 2)
    x1(1, 2)
    x2(1, 1)
    x3(1, 0)
    z_far(1)
    compute(1, 3)
    x1(1, 3)
    x2(1, 2)
    x3(1, 1)
    z_direct(1, 1)
    x2(1, 3)
    x3(1, 2)
    z_direct(1, 2)
    finish(0)
    x3(1, 3)
    z_sum(1, 1)
    z_sum(1, 2)
    finish(1)
    outputs(0)
    outputs(1)
    for d, when in sends:
        if when is None:
            d.wait_send()
        else:
            pl.when(when)(d.wait_send)


def per_device(ancestor, factor_rows, block_lists):
    dma = pltpu.SemaphoreType.DMA
    return pl.pallas_call(
        kernel,
        out_shape=(
            jax.ShapeDtypeStruct((2, 40, 256), F32),
            jax.ShapeDtypeStruct((2, 8, 1280), F32),
        ),
        in_specs=[
            pl.BlockSpec(memory_space=pltpu.SMEM),
            pl.BlockSpec(memory_space=pl.ANY),
            pl.BlockSpec(memory_space=pl.ANY),
        ],
        out_specs=(
            pl.BlockSpec(memory_space=pltpu.VMEM),
            pl.BlockSpec(memory_space=pltpu.VMEM),
        ),
        scratch_shapes=[
            pltpu.VMEM((1280, 1280), F32),
            pltpu.VMEM((1280, 1280), BF16),
            pltpu.VMEM((1280, 1280), BF16),
            pltpu.VMEM((2, 128, 1280), F32),
            pltpu.VMEM((2, 256, 1280), BF16),
            pltpu.VMEM((2, 4, 320, 128), F32),
            pltpu.VMEM((2, 4, 6, 40, 128), F32),
            pltpu.VMEM((2, 6, 40, 128), F32),
            pltpu.VMEM((2, 128, 128), F32),
            pltpu.VMEM((2, 128, 128), F32),
            pltpu.VMEM((2, 16, 8, 128), F32),
            pltpu.VMEM((2, 40, 128), F32),
            dma((4,)),
            dma((4,)),
            dma((4,)),
            dma((2, 8, 2)),
            dma((48,)),
            dma((2, 4, 6)),
            dma((2, 4, 6)),
            dma((2, 6)),
            dma((2, 6)),
            dma((2,)),
            dma((2, 16)),
            dma((2,)),
            dma((2,)),
        ],
        compiler_params=pltpu.CompilerParams(collective_id=0, has_side_effects=True),
    )(block_lists, ancestor, factor_rows)


def solution(mesh):
    in_specs = (P("row", "col"), P(None, "row", "col"), P())
    out_specs = (P(None, ("row", "col"), None), P(None, "col", "row"))
    return jax.shard_map(
        per_device, mesh=mesh, in_specs=in_specs, out_specs=out_specs, check_vma=False
    )
```

```python
import jax
import jax.numpy as jnp
from jax import lax
from jax.experimental import pallas as pl
from jax.experimental.pallas import tpu as pltpu
from jax.sharding import PartitionSpec as P

MESH = pl.DeviceIdType.MESH
F32 = jnp.float32
BF16 = jnp.bfloat16
NT = (((1,), (1,)), ((), ()))
ORDER = (2, 1, 3, 0)


def kernel(
    lists, a_hbm, f_hbm, panel, rows,
    a_v, ah, al, fbuf, fcat, ybuf, xr, zr, tin, tbuf, rbuf, pbuf, ubuf,
    a_sem, ap_sem, ap_send, g_recv, g_send, x_recv, x_send, z_recv, z_send,
    t_recv, t_send, p_recv, p_send,
):
    r = lax.axis_index("row")
    c = lax.axis_index("col")
    zl, y = r // 4, r % 4
    zh, x, k = c // 8, (c // 2) % 4, c % 2
    o_k = 1 - k

    def dev(zl_, y_, zh_, x_, k_):
        return (zl_ * 4 + y_, zh_ * 8 + x_ * 2 + k_)

    partner = dev(zl, y, zh, x, o_k)
    yp, ym = (y + 1) % 4, (y + 3) % 4
    xp, xm, xo = (x + 1) % 4, (x + 3) % 4, (x + 2) % 4
    zp, zm = (zh + 1) % 4, (zh + 3) % 4

    barrier = pltpu.get_barrier_semaphore()
    near = [partner]
    for kk in range(2):
        near += [dev(zl, yp, zh, x, kk), dev(zl, ym, zh, x, kk)]
        near += [dev((zl + t) % 4, y, zh, x, kk) for t in (1, 2, 3)]
    near += [dev(zl, y, zh, xp, k), dev(zl, y, zh, xm, k)]
    near += [dev(zl, y, zp, x, k), dev(zl, y, zm, x, k)]
    for d in near:
        pl.semaphore_signal(barrier, inc=1, device_id=d, device_id_type=MESH)
    pl.semaphore_wait(barrier, len(near))

    sends = []

    def rcopy(src, dst, ssem, rsem, to, when=None):
        d = pltpu.make_async_remote_copy(
            src_ref=src, dst_ref=dst, send_sem=ssem, recv_sem=rsem,
            device_id=to, device_id_type=MESH)
        if when is None:
            d.start()
        else:
            pl.when(when)(d.start)
        sends.append((d, when))
        return d

    def got(dst, sem):
        pltpu.make_async_copy(dst, dst, sem).wait()

    cols_k = pl.ds(pl.multiple_of(k * 640, 128), 640)
    near_z = zl + 1 - 2 * (zl % 2)
    edge = (zl == 0) | (zl == 3)
    others = (near_z, jnp.where(edge, (zl + 2) % 4, 3 - zl), jnp.where(edge, 3 - zl, (zl + 2) % 4))
    g_i = [0]

    def gsem():
        g_i[0] += 1
        return g_send.at[g_i[0] - 1]

    def shard(s, rr):
        return fbuf.at[s, pl.ds(pl.multiple_of(rr * 8, 8), 8), :]

    def half(s, rr, h):
        return fbuf.at[s, pl.ds(pl.multiple_of(rr * 8, 8), 8), pl.ds(h * 640, 640)]

    def first(s, places):
        dst = fbuf.at[s, pl.ds(pl.multiple_of(r * 8, 8), 8), cols_k]
        sem = g_recv.at[s, r, k]
        for zz, yy in places:
            for kk in range(2):
                rcopy(f_hbm.at[s, pl.ds(kk * 8, 8), :], dst, gsem(), sem, dev(zz, yy, zh, x, kk))

    def first_own(s):
        dst = fbuf.at[s, pl.ds(pl.multiple_of(r * 8, 8), 8), cols_k]
        sem = g_recv.at[s, r, k]
        rcopy(f_hbm.at[s, pl.ds(pl.multiple_of(o_k * 8, 8), 8), :], dst, gsem(), sem, partner)
        pltpu.make_async_copy(f_hbm.at[s, pl.ds(pl.multiple_of(k * 8, 8), 8), :], dst, sem).start()

    def first_y(s):
        first(s, ((zl, yp), (zl, ym)))

    def first_z(s):
        first(s, [(zz, y) for zz in others])

    def forward(s, n):
        rr = others[n] * 4 + y
        for h in range(2):
            got(half(s, rr, h), g_recv.at[s, rr, h])
        for yy in (yp, ym):
            rcopy(shard(s, rr), shard(s, rr), gsem(), g_recv.at[s, rr, 0], dev(zl, yy, zh, x, k))

    def relay(s, n):
        zz = zl if n < 0 else others[n]
        for h, (yy, to) in enumerate(((ym, yp), (yp, ym))):
            rr = zz * 4 + yy
            if n < 0:
                got(half(s, rr, 0), g_recv.at[s, rr, 0])
                got(half(s, rr, 1), g_recv.at[s, rr, 1])
            else:
                got(shard(s, rr), g_recv.at[s, rr, 0])
            piece = half(s, rr, h)
            rcopy(piece, piece, gsem(), g_recv.at[s, rr, h], dev(zl, to, zh, x, k))

    def gather_end(s):
        for h in range(2):
            got(half(s, r, h), g_recv.at[s, r, h])
        for zz in (zl,) + others:
            rr = zz * 4 + (y + 2) % 4
            for h in range(2):
                got(half(s, rr, h), g_recv.at[s, rr, h])

    first_y(0)
    first_z(0)
    first_own(0)

    for q in range(4):
        rq = pl.ds(q * 320, 320)
        pltpu.make_async_copy(a_hbm.at[rq, :], a_v.at[rq, cols_k], a_sem.at[q]).start()
        rcopy(a_hbm.at[rq, :], a_v.at[rq, cols_k], ap_send.at[q], ap_sem.at[q], partner)

    first_z(1)
    first_own(1)

    cb = zh * 4 + x

    def listed(s, b):
        hit = lists[s, 0] == b
        for t in range(1, 8):
            hit = jnp.logical_or(hit, lists[s, t] == b)
        return jnp.where(hit, 1.0, 0.0).astype(F32)

    def split_a(q):
        rq = pl.ds(q * 320, 320)
        got(a_v.at[rq, cols_k], a_sem.at[q])
        got(a_v.at[rq, pl.ds(pl.multiple_of(o_k * 640, 128), 640)], ap_sem.at[q])

        def step(t, _):
            at = pl.ds(pl.multiple_of(q * 320 + t * 32, 32), 32)
            v = a_v[at, :]
            hi = v.astype(BF16)
            ah[at, :] = hi
            al[at, :] = (v - hi.astype(F32)).astype(BF16)
            return 0

        lax.fori_loop(0, 10, step, 0)

    def split_f(s):
        mask = listed(s, cb)
        v = fbuf[s] * mask
        hi = v.astype(BF16)
        fcat[s, 0:128, :] = hi
        fcat[s, 128:256, :] = (v - hi.astype(F32)).astype(BF16)

    def compute(s, o):
        zc = (zh + ORDER[o]) % 4
        at = pl.ds(pl.multiple_of(zc * 320, 320), 320)
        sign = -listed(s, r)
        p1 = lax.dot_general(ah[at, :], fcat[s], NT, preferred_element_type=F32)
        p2 = lax.dot_general(al[at, :], fcat[s, 0:128, :], NT, preferred_element_type=F32)
        ybuf[s, o] = (p1[:, 0:128] + (p1[:, 128:256] + p2)) * sign

    def yp_rows(s, o, xx, h):
        return s, o, pl.ds(pl.multiple_of(xx * 80 + h * 40, 8), 40), slice(None)

    to_xp, to_xm = dev(zl, y, zh, xp, k), dev(zl, y, zh, xm, k)
    to_zp, to_zm = dev(zl, y, zp, x, k), dev(zl, y, zm, x, k)

    def xsend(s, o, kind, xx, h, to):
        rcopy(ybuf.at[yp_rows(s, o, xx, h)], xr.at[s, o, kind],
              x_send.at[s, o, kind], x_recv.at[s, o, kind], to)

    def xgot(s, o, kind):
        got(xr.at[s, o, kind], x_recv.at[s, o, kind])

    def x1(s, o):
        xsend(s, o, 0, xo, 0, to_xp)
        xsend(s, o, 1, xo, 1, to_xm)
        xsend(s, o, 4, xp, 1, to_xp)
        xsend(s, o, 5, xm, 0, to_xm)

    def x2(s, o):
        xgot(s, o, 0)
        i = yp_rows(s, o, xp, 0)
        ybuf[i] = ybuf[i] + xr[s, o, 0]
        xsend(s, o, 2, xp, 0, to_xp)
        xgot(s, o, 1)
        i = yp_rows(s, o, xm, 1)
        ybuf[i] = ybuf[i] + xr[s, o, 1]
        xsend(s, o, 3, xm, 1, to_xm)

    def x3(s, o):
        for kinds, h in (((5, 2), 0), ((4, 3), 1)):
            for kind in kinds:
                xgot(s, o, kind)
            i = yp_rows(s, o, x, h)
            ybuf[i] = ybuf[i] + xr[s, o, kinds[0]] + xr[s, o, kinds[1]]

    def zsend(s, o, kind, h, to):
        rcopy(ybuf.at[yp_rows(s, o, x, h)], zr.at[s, kind],
              z_send.at[s, kind], z_recv.at[s, kind], to)

    def zgot(s, kind):
        got(zr.at[s, kind], z_recv.at[s, kind])

    def zadd(s, o, kind, h):
        zgot(s, kind)
        i = yp_rows(s, o, x, h)
        ybuf[i] = ybuf[i] + zr[s, kind]

    def z_far(s):
        zsend(s, 0, 0, 0, to_zp)
        zsend(s, 0, 1, 1, to_zm)

    def z_direct(s, o):
        if o == 1:
            zsend(s, 1, 4, 1, to_zp)
        else:
            zsend(s, 2, 5, 0, to_zm)

    def z_sum(s, o):
        if o == 1:
            zadd(s, 1, 0, 0)
            zsend(s, 1, 2, 0, to_zp)
        else:
            zadd(s, 2, 1, 1)
            zsend(s, 2, 3, 1, to_zm)

    def finish(s):
        for kinds, h in (((5, 2), 0), ((4, 3), 1)):
            for kind in kinds:
                zgot(s, kind)
            v = ybuf[yp_rows(s, 3, x, h)] + zr[s, kinds[0]] + zr[s, kinds[1]]
            tin[s, pl.ds(h * 40, 40), :] = v
        rcopy(tin.at[s, pl.ds(pl.multiple_of(o_k * 40, 8), 40), :], pbuf.at[s],
              p_send.at[s], p_recv.at[s], partner)
        tin[s, 80:128, :] = jnp.zeros((48, 128), F32)
        tbuf[s] = tin[s].T
        for n in range(16):
            nn = (n + cb) % 16
            src = tbuf.at[s, pl.ds(pl.multiple_of(nn * 8, 8), 8), :]
            dst = rbuf.at[s, cb]
            if n:
                rcopy(src, dst, t_send.at[s, n], t_recv.at[s], (r, 2 * nn + k))
            else:
                pltpu.make_async_copy(src, dst, t_recv.at[s]).start()

    def outputs(s):
        got(pbuf.at[s], p_recv.at[s])
        both = jnp.concatenate([
            tin[s, pl.ds(pl.multiple_of(k * 40, 8), 40), :], pbuf[s], jnp.zeros((48, 128), F32)], axis=0).T
        ubuf[s, :, k] = both.reshape(16, 8, 128)
        ubuf[s, :, o_k] = pltpu.roll(both, 88, 1).reshape(16, 8, 128)
        panel[s] = ubuf[s].reshape(256, 128).T[0:40, :]
        got(rbuf.at[s], t_recv.at[s])
        lane = lax.broadcasted_iota(jnp.int32, (8, 128), 1)
        tiles = [jnp.zeros((8, 128), F32) for _ in range(10)]
        for n in range(16):
            t, off = (80 * n) // 128, (80 * n) % 128
            v = rbuf[s, n]
            if off:
                v = pltpu.roll(v, off, 1)
            tiles[t] = jnp.where((lane >= off) & (lane < off + 80), v, tiles[t])
            if off + 80 > 128:
                tiles[t + 1] = jnp.where(lane < off + 80 - 128, v, tiles[t + 1])
        for t in range(10):
            rows[s, :, t * 128:(t + 1) * 128] = tiles[t]

    forward(0, 0)
    split_a(0)
    relay(0, -1)
    forward(0, 1)
    split_a(1)
    relay(0, 0)
    forward(0, 2)
    split_a(2)
    relay(0, 1)
    first_y(1)
    forward(1, 0)
    split_a(3)
    relay(0, 2)
    forward(1, 1)
    relay(1, -1)
    forward(1, 2)
    gather_end(0)
    split_f(0)
    for o in range(4):
        compute(0, o)
        x1(0, o)
        relay(1, 0) if o == 1 else None
    relay(1, 1)
    x2(0, 0)
    x2(0, 1)
    relay(1, 2)
    x2(0, 2)
    x2(0, 3)
    x3(0, 0)
    z_far(0)
    x3(0, 1)
    z_direct(0, 1)
    gather_end(1)
    split_f(1)
    compute(1, 0)
    x1(1, 0)
    compute(1, 1)
    x1(1, 1)
    x3(0, 2)
    z_direct(0, 2)
    compute(1, 2)
    x1(1, 2)
    compute(1, 3)
    x1(1, 3)
    x3(0, 3)
    x2(1, 0)
    x2(1, 1)
    z_sum(0, 1)
    x2(1, 2)
    x2(1, 3)
    z_sum(0, 2)
    x3(1, 0)
    z_far(1)
    x3(1, 1)
    z_direct(1, 1)
    x3(1, 2)
    z_direct(1, 2)
    x3(1, 3)
    finish(0)
    z_sum(1, 1)
    z_sum(1, 2)
    outputs(0)
    finish(1)
    outputs(1)
    for d, when in sends:
        if when is None:
            d.wait_send()
        else:
            pl.when(when)(d.wait_send)


def per_device(ancestor, factor_rows, block_lists):
    dma = pltpu.SemaphoreType.DMA
    return pl.pallas_call(
        kernel,
        out_shape=(
            jax.ShapeDtypeStruct((2, 40, 256), F32),
            jax.ShapeDtypeStruct((2, 8, 1280), F32),
        ),
        in_specs=[
            pl.BlockSpec(memory_space=pltpu.SMEM),
            pl.BlockSpec(memory_space=pl.ANY),
            pl.BlockSpec(memory_space=pl.ANY),
        ],
        out_specs=(
            pl.BlockSpec(memory_space=pltpu.VMEM),
            pl.BlockSpec(memory_space=pltpu.VMEM),
        ),
        scratch_shapes=[
            pltpu.VMEM((1280, 1280), F32),
            pltpu.VMEM((1280, 1280), BF16),
            pltpu.VMEM((1280, 1280), BF16),
            pltpu.VMEM((2, 128, 1280), F32),
            pltpu.VMEM((2, 256, 1280), BF16),
            pltpu.VMEM((2, 4, 320, 128), F32),
            pltpu.VMEM((2, 4, 6, 40, 128), F32),
            pltpu.VMEM((2, 6, 40, 128), F32),
            pltpu.VMEM((2, 128, 128), F32),
            pltpu.VMEM((2, 128, 128), F32),
            pltpu.VMEM((2, 16, 8, 128), F32),
            pltpu.VMEM((2, 40, 128), F32),
            pltpu.VMEM((2, 16, 2, 8, 128), F32),
            dma((4,)),
            dma((4,)),
            dma((4,)),
            dma((2, 16, 2)),
            dma((50,)),
            dma((2, 4, 6)),
            dma((2, 4, 6)),
            dma((2, 6)),
            dma((2, 6)),
            dma((2,)),
            dma((2, 16)),
            dma((2,)),
            dma((2,)),
        ],
        compiler_params=pltpu.CompilerParams(collective_id=0, has_side_effects=True),
    )(block_lists, ancestor, factor_rows)


def solution(mesh):
    in_specs = (P("row", "col"), P(None, "row", "col"), P())
    out_specs = (P(None, ("row", "col"), None), P(None, "col", "row"))
    return jax.shard_map(
        per_device, mesh=mesh, in_specs=in_specs, out_specs=out_specs, check_vma=False
    )
```

```python
import jax
import jax.numpy as jnp
from jax import lax
from jax.experimental import pallas as pl
from jax.experimental.pallas import tpu as pltpu
from jax.sharding import PartitionSpec as P

MESH = pl.DeviceIdType.MESH
F32 = jnp.float32
BF16 = jnp.bfloat16
NT = (((1,), (1,)), ((), ()))
ORDER = (2, 1, 3, 0)


def kernel(
    lists, a_hbm, f_hbm, panel, rows,
    a_v, ah, al, fbuf, fcat, ybuf, xr, zr, tin, tbuf, rbuf, pbuf, ubuf,
    a_sem, ap_sem, ap_send, g_recv, g_send, x_recv, x_send, z_recv, z_send,
    t_recv, t_send, p_recv, p_send, ready,
):
    r = lax.axis_index("row")
    c = lax.axis_index("col")
    zl, y = r // 4, r % 4
    zh, x, k = c // 8, (c // 2) % 4, c % 2
    o_k = 1 - k

    def dev(zl_, y_, zh_, x_, k_):
        return (zl_ * 4 + y_, zh_ * 8 + x_ * 2 + k_)

    partner = dev(zl, y, zh, x, o_k)
    yp, ym = (y + 1) % 4, (y + 3) % 4
    xp, xm, xo = (x + 1) % 4, (x + 3) % 4, (x + 2) % 4
    zp, zm = (zh + 1) % 4, (zh + 3) % 4

    z = zh * 4 + zl

    def zdev(t, kk):
        zz = (z + t) % 16
        return dev(zz % 4, y, zz // 4, x, kk)

    barrier = pltpu.get_barrier_semaphore()
    near = [partner]
    for kk in range(2):
        near += [dev(zl, yp, zh, x, kk), dev(zl, ym, zh, x, kk)]
        near += [zdev(1, kk), zdev(15, kk)]
    near += [dev(zl, y, zh, xp, k), dev(zl, y, zh, xm, k)]
    for d in near:
        pl.semaphore_signal(barrier, inc=1, device_id=d, device_id_type=MESH)
    pl.semaphore_wait(barrier, len(near))

    def tell(stage):
        pl.semaphore_signal(ready.at[0, stage], inc=1, device_id=zdev(1, k), device_id_type=MESH)
        pl.semaphore_signal(ready.at[1, stage], inc=1, device_id=zdev(15, k), device_id_type=MESH)

    def heard(stage):
        pl.semaphore_wait(ready.at[0, stage], 1)
        pl.semaphore_wait(ready.at[1, stage], 1)

    tell(0)
    sends = []

    def rcopy(src, dst, ssem, rsem, to, when=None):
        d = pltpu.make_async_remote_copy(
            src_ref=src, dst_ref=dst, send_sem=ssem, recv_sem=rsem,
            device_id=to, device_id_type=MESH)
        if when is None:
            d.start()
        else:
            pl.when(when)(d.start)
        sends.append((d, when))
        return d

    def got(dst, sem):
        pltpu.make_async_copy(dst, dst, sem).wait()

    cols_k = pl.ds(pl.multiple_of(k * 640, 128), 640)
    near_z = zl + 1 - 2 * (zl % 2)
    edge = (zl == 0) | (zl == 3)
    others = (near_z, jnp.where(edge, (zl + 2) % 4, 3 - zl), jnp.where(edge, 3 - zl, (zl + 2) % 4))
    g_i = [0]

    def gsem():
        g_i[0] += 1
        return g_send.at[g_i[0] - 1]

    def shard(s, rr):
        return fbuf.at[s, pl.ds(pl.multiple_of(rr * 8, 8), 8), :]

    def half(s, rr, h):
        return fbuf.at[s, pl.ds(pl.multiple_of(rr * 8, 8), 8), pl.ds(h * 640, 640)]

    def first(s, places):
        dst = fbuf.at[s, pl.ds(pl.multiple_of(r * 8, 8), 8), cols_k]
        sem = g_recv.at[s, r, k]
        for zz, yy in places:
            for kk in range(2):
                rcopy(f_hbm.at[s, pl.ds(kk * 8, 8), :], dst, gsem(), sem, dev(zz, yy, zh, x, kk))

    def first_own(s):
        dst = fbuf.at[s, pl.ds(pl.multiple_of(r * 8, 8), 8), cols_k]
        sem = g_recv.at[s, r, k]
        rcopy(f_hbm.at[s, pl.ds(pl.multiple_of(o_k * 8, 8), 8), :], dst, gsem(), sem, partner)
        pltpu.make_async_copy(f_hbm.at[s, pl.ds(pl.multiple_of(k * 8, 8), 8), :], dst, sem).start()

    def first_y(s):
        first(s, ((zl, yp), (zl, ym)))

    def first_z(s):
        dst = fbuf.at[s, pl.ds(pl.multiple_of(r * 8, 8), 8), cols_k]
        sem = g_recv.at[s, r, k]
        for zz, ok in ((zl + 1, zl < 3), (zl - 1, zl > 0)):
            for kk in range(2):
                rcopy(f_hbm.at[s, pl.ds(kk * 8, 8), :], dst, gsem(), sem,
                      dev(zz, y, zh, x, kk), when=ok)

    def onward(s, n):
        rr = others[n] * 4 + y
        for h in range(2):
            piece = half(s, rr, h)
            sem = g_recv.at[s, rr, h]
            got(piece, sem)
            rcopy(piece, piece, gsem(), sem, dev(zl + 1, y, zh, x, k),
                  when=(others[n] < zl) & (zl < 3))
            rcopy(piece, piece, gsem(), sem, dev(zl - 1, y, zh, x, k),
                  when=(others[n] > zl) & (zl > 0))

    def spread(s, n):
        rr = others[n] * 4 + y
        for yy in (yp, ym):
            rcopy(shard(s, rr), shard(s, rr), gsem(), g_recv.at[s, rr, 0], dev(zl, yy, zh, x, k))

    def relay(s, n):
        zz = zl if n < 0 else others[n]
        for h, (yy, to) in enumerate(((ym, yp), (yp, ym))):
            rr = zz * 4 + yy
            if n < 0:
                got(half(s, rr, 0), g_recv.at[s, rr, 0])
                got(half(s, rr, 1), g_recv.at[s, rr, 1])
            else:
                got(shard(s, rr), g_recv.at[s, rr, 0])
            piece = half(s, rr, h)
            rcopy(piece, piece, gsem(), g_recv.at[s, rr, h], dev(zl, to, zh, x, k))

    def gather_end(s):
        for h in range(2):
            got(half(s, r, h), g_recv.at[s, r, h])
        for zz in (zl,) + others:
            rr = zz * 4 + (y + 2) % 4
            for h in range(2):
                got(half(s, rr, h), g_recv.at[s, rr, h])

    first_z(0)
    first_y(0)
    first_z(1)
    first_y(1)
    first_own(0)

    for q in range(4):
        rq = pl.ds(q * 320, 320)
        pltpu.make_async_copy(a_hbm.at[rq, :], a_v.at[rq, cols_k], a_sem.at[q]).start()
        rcopy(a_hbm.at[rq, :], a_v.at[rq, cols_k], ap_send.at[q], ap_sem.at[q], partner)

    first_own(1)

    cb = zh * 4 + x

    def listed(s, b):
        hit = lists[s, 0] == b
        for t in range(1, 8):
            hit = jnp.logical_or(hit, lists[s, t] == b)
        return jnp.where(hit, 1.0, 0.0).astype(F32)

    def split_a(q):
        rq = pl.ds(q * 320, 320)
        got(a_v.at[rq, cols_k], a_sem.at[q])
        got(a_v.at[rq, pl.ds(pl.multiple_of(o_k * 640, 128), 640)], ap_sem.at[q])

        def step(t, _):
            at = pl.ds(pl.multiple_of(q * 320 + t * 32, 32), 32)
            v = a_v[at, :]
            hi = v.astype(BF16)
            ah[at, :] = hi
            al[at, :] = (v - hi.astype(F32)).astype(BF16)
            return 0

        lax.fori_loop(0, 10, step, 0)

    def split_f(s):
        mask = listed(s, cb)
        v = fbuf[s] * mask
        hi = v.astype(BF16)
        fcat[s, 0:128, :] = hi
        fcat[s, 128:256, :] = (v - hi.astype(F32)).astype(BF16)

    def compute(s, o):
        zc = (zh + ORDER[o]) % 4
        at = pl.ds(pl.multiple_of(zc * 320, 320), 320)
        sign = -listed(s, r)
        p1 = lax.dot_general(ah[at, :], fcat[s], NT, preferred_element_type=F32)
        p2 = lax.dot_general(al[at, :], fcat[s, 0:128, :], NT, preferred_element_type=F32)
        ybuf[s, o] = (p1[:, 0:128] + (p1[:, 128:256] + p2)) * sign

    def yp_rows(s, o, xx, h):
        return s, o, pl.ds(pl.multiple_of(xx * 80 + h * 40, 8), 40), slice(None)

    to_xp, to_xm = dev(zl, y, zh, xp, k), dev(zl, y, zh, xm, k)
    to_zp, to_zm = dev(zl, y, zp, x, k), dev(zl, y, zm, x, k)

    def xsend(s, o, kind, xx, h, to):
        rcopy(ybuf.at[yp_rows(s, o, xx, h)], xr.at[s, o, kind],
              x_send.at[s, o, kind], x_recv.at[s, o, kind], to)

    def xgot(s, o, kind):
        got(xr.at[s, o, kind], x_recv.at[s, o, kind])

    def x1(s, o):
        xsend(s, o, 0, xo, 0, to_xp)
        xsend(s, o, 1, xo, 1, to_xm)
        xsend(s, o, 4, xp, 1, to_xp)
        xsend(s, o, 5, xm, 0, to_xm)

    def x2(s, o):
        xgot(s, o, 0)
        i = yp_rows(s, o, xp, 0)
        ybuf[i] = ybuf[i] + xr[s, o, 0]
        xsend(s, o, 2, xp, 0, to_xp)
        xgot(s, o, 1)
        i = yp_rows(s, o, xm, 1)
        ybuf[i] = ybuf[i] + xr[s, o, 1]
        xsend(s, o, 3, xm, 1, to_xm)

    def x3(s, o):
        for kinds, h in (((5, 2), 0), ((4, 3), 1)):
            for kind in kinds:
                xgot(s, o, kind)
            i = yp_rows(s, o, x, h)
            ybuf[i] = ybuf[i] + xr[s, o, kinds[0]] + xr[s, o, kinds[1]]

    def zsend(s, o, kind, h, to):
        rcopy(ybuf.at[yp_rows(s, o, x, h)], zr.at[s, kind],
              z_send.at[s, kind], z_recv.at[s, kind], to)

    def zgot(s, kind):
        got(zr.at[s, kind], z_recv.at[s, kind])

    def zadd(s, o, kind, h):
        zgot(s, kind)
        i = yp_rows(s, o, x, h)
        ybuf[i] = ybuf[i] + zr[s, kind]

    def z_far(s):
        zsend(s, 0, 0, 0, to_zp)
        zsend(s, 0, 1, 1, to_zm)

    def z_direct(s, o):
        if o == 1:
            zsend(s, 1, 4, 1, to_zp)
        else:
            zsend(s, 2, 5, 0, to_zm)

    def z_sum(s, o):
        if o == 1:
            zadd(s, 1, 0, 0)
            zsend(s, 1, 2, 0, to_zp)
        else:
            zadd(s, 2, 1, 1)
            zsend(s, 2, 3, 1, to_zm)

    def finish(s):
        for kinds, h in (((5, 2), 0), ((4, 3), 1)):
            for kind in kinds:
                zgot(s, kind)
            v = ybuf[yp_rows(s, 3, x, h)] + zr[s, kinds[0]] + zr[s, kinds[1]]
            tin[s, pl.ds(h * 40, 40), :] = v
        rcopy(tin.at[s, pl.ds(pl.multiple_of(o_k * 40, 8), 40), :], pbuf.at[s],
              p_send.at[s], p_recv.at[s], partner)
        tin[s, 80:128, :] = jnp.zeros((48, 128), F32)
        tbuf[s] = tin[s].T
        for n in range(16):
            nn = (n + cb) % 16
            src = tbuf.at[s, pl.ds(pl.multiple_of(nn * 8, 8), 8), :]
            dst = rbuf.at[s, cb]
            if n:
                rcopy(src, dst, t_send.at[s, n], t_recv.at[s], (r, 2 * nn + k))
            else:
                pltpu.make_async_copy(src, dst, t_recv.at[s]).start()

    def outputs(s):
        got(pbuf.at[s], p_recv.at[s])
        both = jnp.concatenate([
            tin[s, pl.ds(pl.multiple_of(k * 40, 8), 40), :], pbuf[s], jnp.zeros((48, 128), F32)], axis=0).T
        ubuf[s, :, k] = both.reshape(16, 8, 128)
        ubuf[s, :, o_k] = pltpu.roll(both, 88, 1).reshape(16, 8, 128)
        panel[s] = ubuf[s].reshape(256, 128).T[0:40, :]
        got(rbuf.at[s], t_recv.at[s])
        lane = lax.broadcasted_iota(jnp.int32, (8, 128), 1)
        tiles = [jnp.zeros((8, 128), F32) for _ in range(10)]
        for n in range(16):
            t, off = (80 * n) // 128, (80 * n) % 128
            v = rbuf[s, n]
            if off:
                v = pltpu.roll(v, off, 1)
            tiles[t] = jnp.where((lane >= off) & (lane < off + 80), v, tiles[t])
            if off + 80 > 128:
                tiles[t + 1] = jnp.where(lane < off + 80 - 128, v, tiles[t + 1])
        for t in range(10):
            rows[s, :, t * 128:(t + 1) * 128] = tiles[t]

    onward(0, 0)
    spread(0, 0)
    onward(1, 0)
    spread(1, 0)
    heard(0)
    tell(1)
    split_a(0)
    onward(0, 1)
    spread(0, 1)
    onward(1, 1)
    spread(1, 1)
    heard(1)
    tell(2)
    split_a(1)
    onward(0, 2)
    spread(0, 2)
    onward(1, 2)
    spread(1, 2)
    heard(2)
    relay(0, -1)
    relay(1, -1)
    split_a(2)
    relay(0, 0)
    relay(1, 0)
    split_a(3)
    relay(0, 1)
    relay(1, 1)
    relay(0, 2)
    relay(1, 2)
    gather_end(0)
    split_f(0)
    compute(0, 0)
    x1(0, 0)
    compute(0, 1)
    x1(0, 1)
    compute(0, 2)
    x1(0, 2)
    compute(0, 3)
    x1(0, 3)
    gather_end(1)
    split_f(1)
    x2(0, 0)
    compute(1, 0)
    x1(1, 0)
    x2(0, 1)
    compute(1, 1)
    x1(1, 1)
    x2(0, 2)
    x2(0, 3)
    x3(0, 0)
    z_far(0)
    compute(1, 2)
    x1(1, 2)
    x3(0, 1)
    z_direct(0, 1)
    compute(1, 3)
    x1(1, 3)
    x3(0, 2)
    z_direct(0, 2)
    x3(0, 3)
    x2(1, 0)
    x2(1, 1)
    z_sum(0, 1)
    x2(1, 2)
    x2(1, 3)
    z_sum(0, 2)
    x3(1, 0)
    z_far(1)
    x3(1, 1)
    z_direct(1, 1)
    x3(1, 2)
    z_direct(1, 2)
    x3(1, 3)
    finish(0)
    z_sum(1, 1)
    z_sum(1, 2)
    finish(1)
    outputs(0)
    outputs(1)
    for d, when in sends:
        if when is None:
            d.wait_send()
        else:
            pl.when(when)(d.wait_send)


def per_device(ancestor, factor_rows, block_lists):
    dma = pltpu.SemaphoreType.DMA
    return pl.pallas_call(
        kernel,
        out_shape=(
            jax.ShapeDtypeStruct((2, 40, 256), F32),
            jax.ShapeDtypeStruct((2, 8, 1280), F32),
        ),
        in_specs=[
            pl.BlockSpec(memory_space=pltpu.SMEM),
            pl.BlockSpec(memory_space=pltpu.HBM),
            pl.BlockSpec(memory_space=pltpu.HBM),
        ],
        out_specs=(
            pl.BlockSpec(memory_space=pltpu.VMEM),
            pl.BlockSpec(memory_space=pltpu.VMEM),
        ),
        scratch_shapes=[
            pltpu.VMEM((1280, 1280), F32),
            pltpu.VMEM((1280, 1280), BF16),
            pltpu.VMEM((1280, 1280), BF16),
            pltpu.VMEM((2, 128, 1280), F32),
            pltpu.VMEM((2, 256, 1280), BF16),
            pltpu.VMEM((2, 4, 320, 128), F32),
            pltpu.VMEM((2, 4, 6, 40, 128), F32),
            pltpu.VMEM((2, 6, 40, 128), F32),
            pltpu.VMEM((2, 128, 128), F32),
            pltpu.VMEM((2, 128, 128), F32),
            pltpu.VMEM((2, 16, 8, 128), F32),
            pltpu.VMEM((2, 40, 128), F32),
            pltpu.VMEM((2, 16, 2, 8, 128), F32),
            dma((4,)),
            dma((4,)),
            dma((4,)),
            dma((2, 16, 2)),
            dma((70,)),
            dma((2, 4, 6)),
            dma((2, 4, 6)),
            dma((2, 6)),
            dma((2, 6)),
            dma((2,)),
            dma((2, 16)),
            dma((2,)),
            dma((2,)),
            pltpu.SemaphoreType.REGULAR((2, 3)),
        ],
        compiler_params=pltpu.CompilerParams(collective_id=0, has_side_effects=True, vmem_limit_bytes=26 * 1024 * 1024),
    )(block_lists, ancestor, factor_rows)


def solution(mesh):
    in_specs = (P("row", "col"), P(None, "row", "col"), P())
    out_specs = (P(None, ("row", "col"), None), P(None, "col", "row"))
    return jax.shard_map(
        per_device, mesh=mesh, in_specs=in_specs, out_specs=out_specs, check_vma=False
    )
```
